32 devices in a mesh: pipe: 2 (over x), dp: 16 (over z, y, core).
Axes of the slice: x: 2, y: 2, z: 4, core: 2. Of those that a mesh axis runs over, the one named last changes fastest.
Arguments:
- acts: bfloat16 [2, 2048, 8192], P('pipe', 'dp'), may hold values from -6 to 6
- incoming: bfloat16 [2, 2048, 8192], P('pipe', 'dp'), may hold values from -6 to 6
- proj_in: bfloat16 [64, 8192], P(None, 'dp'), may hold values from -0.0625 to 0.0625
- proj_out: bfloat16 [64, 8192], P(None, 'dp'), may hold values from -0.0625 to 0.0625
- valid_rows: bfloat16 [2, 128, 4096], P('pipe', 'dp'), may hold values from -0.09375 to 0.09375
- lengths: int32 [16], P('dp'), may hold values from 1 to 128, 1792 in all
- domains: int32 [16], replicated, may hold values from 0 to 15
Outputs:
- domain_gram: float32 [2, 16, 128, 128], P('pipe', 'dp')
The draws below stay inside these ranges and needn't reach their ends.
All inputs are finite; a program needn't handle non-finite values. No bound on the sum of `lengths` on one device may be relied on, other than what follows from the above.
Results may differ from the reference program's by a relative error of at most 0.004.
Values may be sent and summed in bfloat16 or wider, within the bound.
A program may use at most 128 MiB of HBM per device.

```python
import math
import jax
import jax.numpy as jnp
import numpy as np
from jax import lax

D = 8192
K = 64
KK = 4096
Q = 128
LEN = 128
LAYERS = 2
EXAMPLES = 16
DOMAINS = 16
TOKENS = 2048


def draw_domains(key, part):
    first_key = jax.random.fold_in(key, 11)
    second_key = jax.random.fold_in(key, 12)
    label_key = jax.random.fold_in(key, 13)
    place_key = jax.random.fold_in(key, 14)
    first_pick = jax.random.randint(first_key, (EXAMPLES,), 0, DOMAINS, dtype=jnp.int32)
    second_pick = jax.random.randint(second_key, (EXAMPLES,), 0, DOMAINS, dtype=jnp.int32)
    labels = jax.random.permutation(label_key, DOMAINS).astype(jnp.int32)
    picked = labels[jnp.minimum(first_pick, second_pick)]
    first_slot = jax.random.randint(place_key, (), 0, EXAMPLES, dtype=jnp.int32)
    second_slot = (first_slot + EXAMPLES // 2) % EXAMPLES
    slots = jnp.arange(EXAMPLES, dtype=jnp.int32)
    picked = jnp.where(slots == first_slot, DOMAINS - 1, picked)
    picked = jnp.where(slots == second_slot, 0, picked)
    return picked.astype(jnp.int32)


def steps_of(rng, shape, shards, least, high):
    def one(position, blocks):
        heights = jax.random.uniform(jax.random.fold_in(jax.random.fold_in(rng, 6), position), (blocks,), jnp.float32, least / len(shards), high / len(shards))
        return jnp.repeat(jnp.exp(heights), shape[position] // blocks).reshape((-1,) + (1,) * (len(shape) - position - 1))

    loudness = one(*shards[0])
    for cut in shards[1:]:
        loudness = loudness * one(*cut)
    return loudness


def profile(amount, total, limit, slope):
    portions = [(1 << 20) // math.isqrt(rank ** slope) + 1 for rank in range(2, amount + 1)]
    surplus, given = total - limit - (amount - 1), [1] * (amount - 1)
    while surplus > 0:
        free = [i for i in range(amount - 1) if given[i] < limit]
        pool, budget = sum([portions[i] for i in free]), surplus
        for i in free:
            more = min(limit - given[i], max(1, budget * portions[i] // pool), surplus)
            given[i] = given[i] + more
            surplus = surplus - more
    return np.array([limit] + given)


def uneven(rng, count, total, reach, slope):
    if count == 2:
        one = jax.random.randint(rng, (), max(1, total - reach), min(reach, total - 1) + 1)
        return jnp.stack([one, total - one])
    tallies = jnp.asarray(profile(count, total, reach, slope), jnp.int32)
    pairs = (count - 1) // 2
    source_of, receiver = tallies[1:1 + 2 * pairs:2], tallies[2:2 + 2 * pairs:2]
    slack = jnp.minimum(source_of - 1, reach - receiver)
    passed = jax.random.randint(jax.random.fold_in(rng, 1), (pairs,), 0, 1 << 20) % (slack + 1)
    tallies = tallies.at[1:1 + 2 * pairs:2].set(source_of - passed).at[2:2 + 2 * pairs:2].set(receiver + passed)
    return tallies[jax.random.permutation(jax.random.fold_in(rng, 2), count)]


def scatter_about(stream_key, shape, width, most, split=(), held_as=jnp.bfloat16):
    loudness = steps_of(stream_key, shape, split, -0.22, 0.18) if split else 1.0
    drawn = jax.random.normal(stream_key, shape, jnp.float32) * width * loudness
    return jnp.minimum(jnp.maximum(drawn, -most), most).astype(held_as)


def setup_inputs(seed: int = 0) -> dict:
    streams_of = jax.random.split(jax.random.key(seed), 8)
    acts = scatter_about(streams_of[0], (LAYERS, TOKENS, D), 1.0, 6.0, ((0, 2), (1, 16)))
    incoming = scatter_about(streams_of[1], (LAYERS, TOKENS, D), 1.0, 6.0, ((0, 2), (1, 16)))
    proj_in = scatter_about(streams_of[2], (K, D), D ** -0.5, 0.0625, ((1, 16),))
    proj_out = scatter_about(streams_of[3], (K, D), D ** -0.5, 0.0625, ((1, 16),))
    valid_rows = scatter_about(streams_of[4], (LAYERS, Q, KK), KK ** -0.5, 0.09375, ((0, 2), (1, 16)))
    lengths = uneven(streams_of[5], EXAMPLES, 7 * EXAMPLES * LEN // 8, LEN, 0).astype(jnp.int32)
    domains = draw_domains(jax.random.fold_in(streams_of[7], 71), 0)
    return dict(acts=acts, incoming=incoming, proj_in=proj_in, proj_out=proj_out, valid_rows=valid_rows, lengths=lengths, domains=domains)


highest_precision = lax.Precision.HIGHEST


def reference(acts, incoming, proj_in, proj_out, valid_rows, lengths, domains):
    count_ex = lengths.shape[0]
    positions = jnp.arange(LEN, dtype=jnp.int32)
    live = (positions[None, :] < lengths[:, None]).astype(jnp.float32)
    weights = live / lengths[:, None].astype(jnp.float32)
    owners = (domains[:, None] == jnp.arange(DOMAINS, dtype=jnp.int32)[None, :]).astype(jnp.float32)
    out_f32 = proj_out.astype(jnp.float32)

    def per_layer(carry, layer_in):
        layer_act, branch, valid = layer_in
        grad = carry + branch.astype(jnp.float32)
        proj_act = jnp.dot(layer_act, proj_in.T, preferred_element_type=jnp.float32)
        proj_grad = jnp.dot(grad, out_f32.T, precision=highest_precision)
        scaled = proj_grad.reshape(count_ex, LEN, K) * weights[:, :, None]
        rows = jnp.einsum("eta,etb->eab", scaled, proj_act.reshape(count_ex, LEN, K), precision=highest_precision)
        rows = rows.reshape(count_ex, K * K).astype(jnp.bfloat16)
        scores = jnp.dot(rows, valid.T, preferred_element_type=jnp.float32)
        outer = jnp.einsum("eq,er->eqr", scores, scores, precision=highest_precision)
        gram = jnp.einsum("ed,eqr->dqr", owners, outer, precision=highest_precision)
        return grad, gram

    start_grad = jnp.zeros((TOKENS, D), jnp.float32)
    final_grad, grams = lax.scan(per_layer, start_grad, (acts, incoming, valid_rows), reverse=True)
    return grams
```

```python
import functools

import jax
import jax.numpy as jnp
from jax import lax
from jax.experimental import pallas as pl
from jax.experimental.pallas import tpu as pltpu
from jax.sharding import PartitionSpec as P

MESH = pl.DeviceIdType.MESH
HIGHEST = lax.Precision.HIGHEST
CORES = 2
SIDES = 2
GROUP = CORES * SIDES


def kernel(
    stages, dp,
    acts_hbm, inc_hbm, pin_hbm, pout_hbm, valid_hbm, lengths, domains,
    gram_ref,
    acts, inc, pout, pin, valid, valid_full, grad_acc, act_acc, higher, wide, scores, flat, kept,
    load_sem, send_sem, recv_sem, pipe_send, pipe_recv, score_send, score_recv,
):
    stage = lax.axis_index("pipe")
    me = lax.axis_index("dp")
    line_len = dp // GROUP
    line = me // GROUP
    side = (me // CORES) % SIDES
    core = me % CORES
    hbm = (pout_hbm, pin_hbm, valid_hbm.at[0])
    bufs = (pout, pin, valid)

    def at(z, y, c):
        return z * GROUP + y * CORES + c

    loads = [pltpu.make_async_copy(hbm[a], bufs[a].at[me], load_sem.at[a]) for a in range(3)]
    loads.append(pltpu.make_async_copy(inc_hbm.at[0], inc, load_sem.at[3]))
    loads.append(pltpu.make_async_copy(acts_hbm.at[0], acts, load_sem.at[4]))
    for copy in loads:
        copy.start()

    barrier = pltpu.get_barrier_semaphore()
    for k in range(1, dp):
        pl.semaphore_signal(barrier, inc=1, device_id=(stage, (me + k) % dp), device_id_type=MESH)
    for k in range(1, stages):
        pl.semaphore_signal(barrier, inc=1, device_id=((stage + k) % stages, me), device_id_type=MESH)
    grad_acc[...] = jnp.zeros_like(grad_acc)
    act_acc[...] = jnp.zeros_like(act_acc)
    pl.semaphore_wait(barrier, dp + stages - 2)

    up, down, over, across = 0, 1, 2, 3
    targets = (
        at(line + 1, side, core),
        at(line - 1, side, core),
        at(line, 1 - side, core),
        at(line, side, 1 - core),
    )

    def copy_of(a, shard, way):
        return pltpu.make_async_remote_copy(
            src_ref=bufs[a].at[shard],
            dst_ref=bufs[a].at[shard],
            send_sem=send_sem.at[a, way, shard],
            recv_sem=recv_sem.at[a, shard],
            device_id=(stage, targets[way]),
            device_id_type=MESH,
        )

    def arrived(a, shard):
        copy_of(a, shard, across).wait_recv()

    def line_stage(a, d):
        if d == 0:
            loads[a].wait()

            @pl.when(line < line_len - 1)
            def _():
                copy_of(a, me, up).start()

            @pl.when(line > 0)
            def _():
                copy_of(a, me, down).start()

            copy_of(a, me, over).start()
            copy_of(a, me, across).start()
            return
        for way, sign in ((up, -1), (down, 1)):
            source = line + sign * d

            @pl.when((source >= 0) & (source < line_len))
            def _(source=source, way=way):
                shard = at(source, side, core)
                arrived(a, shard)
                more = (line < line_len - 1) if way == up else (line > 0)

                @pl.when(more)
                def _():
                    copy_of(a, shard, way).start()

                copy_of(a, shard, over).start()
                copy_of(a, shard, across).start()

    def sources_of(d):
        if d == 0:
            return [(line, None)]
        return [
            (line + s * d, (line + s * d >= 0) & (line + s * d < line_len)) for s in (-1, 1)
        ]

    def guarded(d, what):
        for source, ok in sources_of(d):
            if ok is None:
                what(source)
            else:
                pl.when(ok)(functools.partial(what, source))

    def side_stage(a, d):
        def one(source):
            shard = at(source, 1 - side, core)
            arrived(a, shard)
            copy_of(a, shard, across).start()

        guarded(d, one)

    def core_stage(a, d):
        def one(source):
            arrived(a, at(source, side, 1 - core))
            arrived(a, at(source, 1 - side, 1 - core))
            base = source * GROUP
            if a == 2:
                rows = valid.shape[1] * GROUP
                part = valid[pl.ds(base, GROUP)].astype(jnp.float32)
                valid_full[pl.ds(pl.multiple_of(source * rows, rows), rows)] = part.reshape(
                    rows, valid.shape[2]
                ).astype(jnp.bfloat16)
                return
            acc, data, buf = (grad_acc, inc, pout) if a == 0 else (act_acc, acts, pin)
            width = buf.shape[2]
            total = acc[...]
            for j in range(GROUP):
                columns = pl.ds(pl.multiple_of((base + j) * width, width), width)
                total += lax.dot_general(
                    buf[base + j], data[:, columns], (((1,), (1,)), ((), ())),
                    preferred_element_type=jnp.float32,
                )
            acc[...] = total

        if d == 0 and a < 2:
            loads[3 + a].wait()
        guarded(d, one)

    def pipe_copy(k):
        return pltpu.make_async_remote_copy(
            src_ref=grad_acc,
            dst_ref=higher.at[k - 1],
            send_sem=pipe_send.at[k - 1],
            recv_sem=pipe_recv.at[k - 1],
            device_id=(stage - k, me),
            device_id_type=MESH,
        )

    steps = [(a, d) for a in range(3) for d in range(line_len)]
    for t in range(len(steps) + 2):
        if t < len(steps):
            line_stage(*steps[t])
        if 1 <= t < len(steps) + 1:
            side_stage(*steps[t - 1])
        if t >= 2:
            core_stage(*steps[t - 2])
            if steps[t - 2] == (0, line_len - 1):
                for k in range(1, stages):
                    @pl.when(stage >= k)
                    def _(k=k):
                        pipe_copy(k).start()

    grad = grad_acc[...]
    for k in range(1, stages):
        @pl.when(stage + k < stages)
        def _(k=k):
            pipe_copy(k).wait_recv()

        grad += jnp.where(stage + k < stages, higher[k - 1], 0.0)
    tokens = grad.shape[1]
    size = grad.shape[0]
    live = lengths[0]
    positions = lax.broadcasted_iota(jnp.int32, (1, tokens), 1)
    weights = jnp.where(positions < live, 1.0, 0.0) / jnp.full(
        (1, tokens), live.astype(jnp.float32), jnp.float32
    )
    scaled = grad * weights
    act = act_acc[...]
    row = lax.dot_general(
        scaled, jnp.concatenate([act, act], axis=0), (((1,), (1,)), ((), ())),
        precision=HIGHEST, preferred_element_type=jnp.float32,
    )
    a_index = lax.broadcasted_iota(jnp.int32, (size, 2 * size), 0)
    half = lax.broadcasted_iota(jnp.int32, (size, 2 * size), 1) // size
    for k in range(size // 2):
        wide[:, 2 * size * k : 2 * size * (k + 1)] = jnp.where(
            a_index == 2 * k + half, row, 0.0
        ).astype(jnp.bfloat16)
    terms = lax.dot_general(
        wide[...], valid_full[...], (((1,), (1,)), ((), ())), preferred_element_type=jnp.float32
    )
    scores[me] = jnp.sum(terms, axis=0, keepdims=True)

    def score_copy(k):
        return pltpu.make_async_remote_copy(
            src_ref=scores.at[me],
            dst_ref=scores.at[me],
            send_sem=score_send.at[k],
            recv_sem=score_recv.at[me],
            device_id=(stage, (me + k) % dp),
            device_id_type=MESH,
        )

    for k in range(1, dp):
        score_copy(k).start()
    for k in range(1, dp):
        peer = (me + k) % dp
        pltpu.make_async_remote_copy(
            src_ref=scores.at[peer],
            dst_ref=scores.at[peer],
            send_sem=score_send.at[k],
            recv_sem=score_recv.at[peer],
            device_id=(stage, peer),
            device_id_type=MESH,
        ).wait_recv()
    for e in range(dp):
        line_e = scores[e]
        flat[e : e + 1, :] = line_e
        kept[e : e + 1, :] = line_e * jnp.where(domains[e] == me, 1.0, 0.0)
    gram_ref[0, 0] = lax.dot_general(
        kept[...], flat[...], (((0,), (0,)), ((), ())), precision=HIGHEST,
        preferred_element_type=jnp.float32,
    )

    for k in range(1, dp):
        score_copy(k).wait_send()
    for k in range(1, stages):
        @pl.when(stage >= k)
        def _(k=k):
            pipe_copy(k).wait_send()

    for a, d in steps:
        def sent(source, a=a, d=d):
            mine = at(source, side, core)
            if d == 0:
                pl.when(line < line_len - 1)(lambda: copy_of(a, mine, up).wait_send())
                pl.when(line > 0)(lambda: copy_of(a, mine, down).wait_send())
            else:
                pl.when((source < line) & (line < line_len - 1))(
                    lambda: copy_of(a, mine, up).wait_send()
                )
                pl.when((source > line) & (line > 0))(lambda: copy_of(a, mine, down).wait_send())
            copy_of(a, mine, over).wait_send()
            copy_of(a, mine, across).wait_send()
            copy_of(a, at(source, 1 - side, core), across).wait_send()

        guarded(d, sent)


def solution(mesh):
    stages, dp = mesh.shape["pipe"], mesh.shape["dp"]

    def body(acts, incoming, proj_in, proj_out, valid_rows, lengths, domains):
        tokens, wide = acts.shape[1:]
        size, shard = proj_in.shape
        held, entries = valid_rows.shape[1:]
        queries = held * dp
        any_spec = pl.BlockSpec(memory_space=pl.ANY)
        smem = pl.BlockSpec(memory_space=pltpu.SMEM)
        f32, bf16 = jnp.float32, jnp.bfloat16
        dma = pltpu.SemaphoreType.DMA
        return pl.pallas_call(
            functools.partial(kernel, stages, dp),
            out_shape=jax.ShapeDtypeStruct((1, 1, queries, queries), f32),
            in_specs=[any_spec] * 5 + [smem] * 2,
            out_specs=pl.BlockSpec(memory_space=pltpu.VMEM),
            scratch_shapes=[
                pltpu.VMEM((tokens, wide), bf16),
                pltpu.VMEM((tokens, wide), bf16),
                pltpu.VMEM((dp, size, shard), bf16),
                pltpu.VMEM((dp, size, shard), bf16),
                pltpu.VMEM((dp, held, entries), bf16),
                pltpu.VMEM((queries, entries), bf16),
                pltpu.VMEM((size, tokens), f32),
                pltpu.VMEM((size, tokens), f32),
                pltpu.VMEM((max(stages - 1, 1), size, tokens), f32),
                pltpu.VMEM((size, entries), bf16),
                pltpu.VMEM((dp, 1, queries), f32),
                pltpu.VMEM((dp, queries), f32),
                pltpu.VMEM((dp, queries), f32),
                dma((5,)),
                dma((3, 4, dp)),
                dma((3, dp)),
                dma((max(stages - 1, 1),)),
                dma((max(stages - 1, 1),)),
                dma((dp,)),
                dma((dp,)),
            ],
            compiler_params=pltpu.CompilerParams(collective_id=0, has_side_effects=True),
        )(acts, incoming, proj_in, proj_out, valid_rows, lengths, domains)

    placed = (
        P("pipe", "dp", None),
        P("pipe", "dp", None),
        P(None, "dp"),
        P(None, "dp"),
        P("pipe", "dp", None),
        P("dp"),
        P(),
    )
    return jax.shard_map(
        body, mesh=mesh, in_specs=placed, out_specs=P("pipe", "dp", None, None), check_vma=False
    )
```

```python
import functools

import jax
import jax.numpy as jnp
from jax import lax
from jax.experimental import pallas as pl
from jax.experimental.pallas import tpu as pltpu
from jax.sharding import PartitionSpec as P

MESH = pl.DeviceIdType.MESH
HIGHEST = lax.Precision.HIGHEST
CORES = 2
SIDES = 2
GROUP = CORES * SIDES
REACH = 1
LINE_STEPS = (1, -1)
SPLIT = True
LAGS = (3, 5, 6)


def turn(step):
    a, d = step
    return 2 * a + d + 1.5 * ((d - 1) // REACH) if d else a - 5


def kernel(
    stages, dp,
    acts_hbm, inc_hbm, pin_hbm, pout_hbm, valid_hbm, lengths, domains,
    gram_ref,
    acts, inc, pout, pin, valid, valid_full, grad_acc, act_acc, higher, wide, scores, flat, kept,
    load_sem, send_sem, recv_sem, pipe_send, pipe_recv, score_send, score_recv,
):
    stage = lax.axis_index("pipe")
    me = lax.axis_index("dp")
    line_len = dp // GROUP
    line = me // GROUP
    side = (me // CORES) % SIDES
    core = me % CORES
    hbm = (pout_hbm, pin_hbm, valid_hbm.at[0])
    bufs = (pout, pin, valid)

    def at(z, y, c):
        return z * GROUP + y * CORES + c

    loads = [pltpu.make_async_copy(hbm[a], bufs[a].at[me], load_sem.at[a]) for a in range(3)]
    loads.append(pltpu.make_async_copy(inc_hbm.at[0], inc, load_sem.at[3]))
    loads.append(pltpu.make_async_copy(acts_hbm.at[0], acts, load_sem.at[4]))
    for copy in loads:
        copy.start()

    barrier = pltpu.get_barrier_semaphore()
    heard = jnp.int32(2 + stages - 1)
    near = [((stage, at(line, 1 - side, core)), None), ((stage, at(line, side, 1 - core)), None)]
    near += [(((stage + k) % stages, me), None) for k in range(1, stages)]
    for step in LINE_STEPS:
        here = line + step
        near.append(((stage, at(here, side, core)), (here >= 0) & (here < line_len)))
    for device, ok in near:
        def greet(device=device):
            pl.semaphore_signal(barrier, inc=1, device_id=device, device_id_type=MESH)

        if ok is None:
            greet()
        else:
            pl.when(ok)(greet)
            heard += ok.astype(jnp.int32)
    grad_acc[...] = jnp.zeros_like(grad_acc)
    act_acc[...] = jnp.zeros_like(act_acc)
    pl.semaphore_wait(barrier, heard)

    over, across, cross = range(len(LINE_STEPS), len(LINE_STEPS) + 3)
    other_stage = stage + 1 - 2 * (stage % 2)
    targets = tuple((stage, at(line + step, side, core)) for step in LINE_STEPS) + (
        (stage, at(line, 1 - side, core)),
        (stage, at(line, side, 1 - core)),
        (other_stage, me),
    )

    def copy_of(a, shard, way, receiving=False):
        ref = bufs[a].at[shard]
        if way in (over, cross) and shared(a):
            half = stage % 2
            if receiving and way == cross:
                half = 1 - half
            rows = bufs[a].shape[1] // 2
            ref = bufs[a].at[shard, pl.ds(pl.multiple_of(half * rows, rows), rows)]
        return pltpu.make_async_remote_copy(
            src_ref=ref,
            dst_ref=ref,
            send_sem=send_sem.at[a, way, shard],
            recv_sem=recv_sem.at[a, 1 if way == cross else 0, shard],
            device_id=targets[way],
            device_id_type=MESH,
        )

    def shared(a):
        return SPLIT and a < 2 and stages % 2 == 0

    def arrived(a, shard, way=across):
        copy_of(a, shard, way, True).wait_recv()

    def along_line(a, source, d, act):
        shard = at(source, side, core)
        for way, step in enumerate(LINE_STEPS):
            here = line + step
            ok = (here >= 0) & (here < line_len)
            if d:
                ok = ok & ((source < line) if step > 0 else (source > line))

            @pl.when(ok)
            def _(way=way):
                act(copy_of(a, shard, way))

    def line_stage(a, d):
        if d == 0:
            loads[a].wait()
        def one(source):
            shard = at(source, side, core)
            if d:
                arrived(a, shard)
            if d % REACH == 0:
                along_line(a, source, d, lambda copy: copy.start())
            copy_of(a, shard, over).start()
            copy_of(a, shard, across).start()

        guarded(d, one)

    def sources_of(d):
        if d == 0:
            return [(line, None)]
        return [
            (line + s * d, (line + s * d >= 0) & (line + s * d < line_len)) for s in (-1, 1)
        ]

    def guarded(d, what):
        for source, ok in sources_of(d):
            if ok is None:
                what(source)
            else:
                pl.when(ok)(functools.partial(what, source))

    def side_stage(a, d):
        def one(source):
            shard = at(source, 1 - side, core)
            arrived(a, shard, over)
            copy_of(a, shard, cross if shared(a) else across).start()

        guarded(d, one)

    def cross_stage(a, d):
        def one(source):
            shard = at(source, 1 - side, core)
            arrived(a, shard, cross)
            copy_of(a, shard, across).start()

        if shared(a):
            guarded(d, one)

    def core_stage(a, d):
        def one(source):
            arrived(a, at(source, side, 1 - core))
            arrived(a, at(source, 1 - side, 1 - core))
            base = source * GROUP
            if a == 2:
                rows = valid.shape[1] * GROUP
                part = valid[pl.ds(base, GROUP)].astype(jnp.float32)
                valid_full[pl.ds(pl.multiple_of(source * rows, rows), rows)] = part.reshape(
                    rows, valid.shape[2]
                ).astype(jnp.bfloat16)
                return
            acc, data, buf = (grad_acc, inc, pout) if a == 0 else (act_acc, acts, pin)
            width = buf.shape[2]
            total = acc[...]
            for j in range(GROUP):
                columns = pl.ds(pl.multiple_of((base + j) * width, width), width)
                total += lax.dot_general(
                    buf[base + j], data[:, columns], (((1,), (1,)), ((), ())),
                    preferred_element_type=jnp.float32,
                )
            acc[...] = total

        if d == 0 and a < 2:
            loads[3 + a].wait()
        guarded(d, one)

    def pipe_copy(k):
        return pltpu.make_async_remote_copy(
            src_ref=grad_acc,
            dst_ref=higher.at[k - 1],
            send_sem=pipe_send.at[k - 1],
            recv_sem=pipe_recv.at[k - 1],
            device_id=(stage - k, me),
            device_id_type=MESH,
        )

    steps = [(a, d) for a in range(3) for d in range(line_len)]
    steps.sort(key=turn)
    for t in range(len(steps) + LAGS[2]):
        if t < len(steps):
            line_stage(*steps[t])
        if 0 <= t - LAGS[0] < len(steps):
            side_stage(*steps[t - LAGS[0]])
        if 0 <= t - LAGS[1] < len(steps):
            cross_stage(*steps[t - LAGS[1]])
        if t >= LAGS[2]:
            core_stage(*steps[t - LAGS[2]])
            if steps[t - LAGS[2]] == (0, line_len - 1):
                for k in range(1, stages):
                    @pl.when(stage >= k)
                    def _(k=k):
                        pipe_copy(k).start()

    grad = grad_acc[...]
    for k in range(1, stages):
        @pl.when(stage + k < stages)
        def _(k=k):
            pipe_copy(k).wait_recv()

        grad += jnp.where(stage + k < stages, higher[k - 1], 0.0)
    tokens = grad.shape[1]
    size = grad.shape[0]
    live = lengths[0]
    positions = lax.broadcasted_iota(jnp.int32, (1, tokens), 1)
    weights = jnp.where(positions < live, 1.0, 0.0) / jnp.full(
        (1, tokens), live.astype(jnp.float32), jnp.float32
    )
    scaled = grad * weights
    act = act_acc[...]
    row = lax.dot_general(
        scaled, jnp.concatenate([act, act], axis=0), (((1,), (1,)), ((), ())),
        precision=HIGHEST, preferred_element_type=jnp.float32,
    )
    a_index = lax.broadcasted_iota(jnp.int32, (size, 2 * size), 0)
    half = lax.broadcasted_iota(jnp.int32, (size, 2 * size), 1) // size
    for k in range(size // 2):
        wide[:, 2 * size * k : 2 * size * (k + 1)] = jnp.where(
            a_index == 2 * k + half, row, 0.0
        ).astype(jnp.bfloat16)
    terms = lax.dot_general(
        wide[...], valid_full[...], (((1,), (1,)), ((), ())), preferred_element_type=jnp.float32
    )
    scores[me] = jnp.sum(terms, axis=0, keepdims=True)

    def score_copy(k):
        return pltpu.make_async_remote_copy(
            src_ref=scores.at[me],
            dst_ref=scores.at[me],
            send_sem=score_send.at[k],
            recv_sem=score_recv.at[me],
            device_id=(stage, (me + k) % dp),
            device_id_type=MESH,
        )

    for k in range(1, dp):
        score_copy(k).start()
    for k in range(1, dp):
        peer = (me + k) % dp
        pltpu.make_async_remote_copy(
            src_ref=scores.at[peer],
            dst_ref=scores.at[peer],
            send_sem=score_send.at[k],
            recv_sem=score_recv.at[peer],
            device_id=(stage, peer),
            device_id_type=MESH,
        ).wait_recv()
    for e in range(dp):
        line_e = scores[e]
        flat[e : e + 1, :] = line_e
        kept[e : e + 1, :] = line_e * jnp.where(domains[e] == me, 1.0, 0.0)
    gram_ref[0, 0] = lax.dot_general(
        kept[...], flat[...], (((0,), (0,)), ((), ())), precision=HIGHEST,
        preferred_element_type=jnp.float32,
    )

    for k in range(1, dp):
        score_copy(k).wait_send()
    for k in range(1, stages):
        @pl.when(stage >= k)
        def _(k=k):
            pipe_copy(k).wait_send()

    for a, d in steps:
        def sent(source, a=a, d=d):
            mine = at(source, side, core)
            beside = at(source, 1 - side, core)
            if d % REACH == 0:
                along_line(a, source, d, lambda copy: copy.wait_send())
            copy_of(a, mine, over).wait_send()
            copy_of(a, mine, across).wait_send()
            if shared(a):
                copy_of(a, beside, cross).wait_send()
            copy_of(a, beside, across).wait_send()

        guarded(d, sent)


def solution(mesh):
    stages, dp = mesh.shape["pipe"], mesh.shape["dp"]

    def body(acts, incoming, proj_in, proj_out, valid_rows, lengths, domains):
        tokens, wide = acts.shape[1:]
        size, shard = proj_in.shape
        held, entries = valid_rows.shape[1:]
        queries = held * dp
        any_spec = pl.BlockSpec(memory_space=pl.ANY)
        smem = pl.BlockSpec(memory_space=pltpu.SMEM)
        f32, bf16 = jnp.float32, jnp.bfloat16
        dma = pltpu.SemaphoreType.DMA
        return pl.pallas_call(
            functools.partial(kernel, stages, dp),
            out_shape=jax.ShapeDtypeStruct((1, 1, queries, queries), f32),
            in_specs=[any_spec] * 5 + [smem] * 2,
            out_specs=pl.BlockSpec(memory_space=pltpu.VMEM),
            scratch_shapes=[
                pltpu.VMEM((tokens, wide), bf16),
                pltpu.VMEM((tokens, wide), bf16),
                pltpu.VMEM((dp, size, shard), bf16),
                pltpu.VMEM((dp, size, shard), bf16),
                pltpu.VMEM((dp, held, entries), bf16),
                pltpu.VMEM((queries, entries), bf16),
                pltpu.VMEM((size, tokens), f32),
                pltpu.VMEM((size, tokens), f32),
                pltpu.VMEM((max(stages - 1, 1), size, tokens), f32),
                pltpu.VMEM((size, entries), bf16),
                pltpu.VMEM((dp, 1, queries), f32),
                pltpu.VMEM((dp, queries), f32),
                pltpu.VMEM((dp, queries), f32),
                dma((5,)),
                dma((3, len(LINE_STEPS) + 3, dp)),
                dma((3, 2, dp)),
                dma((max(stages - 1, 1),)),
                dma((max(stages - 1, 1),)),
                dma((dp,)),
                dma((dp,)),
            ],
            compiler_params=pltpu.CompilerParams(collective_id=0, has_side_effects=True),
        )(acts, incoming, proj_in, proj_out, valid_rows, lengths, domains)

    placed = (
        P("pipe", "dp", None),
        P("pipe", "dp", None),
        P(None, "dp"),
        P(None, "dp"),
        P("pipe", "dp", None),
        P("dp"),
        P(),
    )
    return jax.shard_map(
        body, mesh=mesh, in_specs=placed, out_specs=P("pipe", "dp", None, None), check_vma=False
    )
```

```python
import functools

import jax
import jax.numpy as jnp
from jax import lax
from jax.experimental import pallas as pl
from jax.experimental.pallas import tpu as pltpu
from jax.sharding import PartitionSpec as P

MESH = pl.DeviceIdType.MESH
HIGHEST = lax.Precision.HIGHEST
CORES = 2
SIDES = 2
GROUP = CORES * SIDES
REACH = 1
LINE_STEPS = (1, -1)
SPLIT = (2, 2, 0)
FIRST, LAP, OVER, CROSS, ACROSS = 2, 3, 4, 4, 3


def turn(step, split, kind):
    a, d = step
    start = FIRST + a + LAP * (d - 1) if d else a - 9
    waits = (0, OVER, OVER + (CROSS if split else 0), OVER + (CROSS if split else 0) + ACROSS)
    return max(start, 0 if kind else -9) + waits[kind]


def kernel(
    stages, dp,
    acts_hbm, inc_hbm, pin_hbm, pout_hbm, valid_hbm, lengths, domains,
    gram_ref,
    acts, inc, pout, pin, valid, valid_full, grad_acc, act_acc, higher, wide, scores, flat, kept,
    load_sem, send_sem, recv_sem, pipe_send, pipe_recv, score_send, score_recv,
):
    stage = lax.axis_index("pipe")
    me = lax.axis_index("dp")
    line_len = dp // GROUP
    line = me // GROUP
    side = (me // CORES) % SIDES
    core = me % CORES
    hbm = (pout_hbm, pin_hbm, valid_hbm.at[0])
    bufs = (pout, pin, valid)

    def at(z, y, c):
        return z * GROUP + y * CORES + c

    loads = [pltpu.make_async_copy(hbm[a], bufs[a].at[me], load_sem.at[a]) for a in range(3)]
    loads.append(pltpu.make_async_copy(inc_hbm.at[0], inc, load_sem.at[3]))
    loads.append(pltpu.make_async_copy(acts_hbm.at[0], acts, load_sem.at[4]))
    for copy in loads:
        copy.start()

    barrier = pltpu.get_barrier_semaphore()
    heard = jnp.int32(2 + stages - 1)
    near = [((stage, at(line, 1 - side, core)), None), ((stage, at(line, side, 1 - core)), None)]
    near += [(((stage + k) % stages, me), None) for k in range(1, stages)]
    for step in LINE_STEPS:
        here = line + step
        near.append(((stage, at(here, side, core)), (here >= 0) & (here < line_len)))
    for device, ok in near:
        def greet(device=device):
            pl.semaphore_signal(barrier, inc=1, device_id=device, device_id_type=MESH)

        if ok is None:
            greet()
        else:
            pl.when(ok)(greet)
            heard += ok.astype(jnp.int32)
    grad_acc[...] = jnp.zeros_like(grad_acc)
    act_acc[...] = jnp.zeros_like(act_acc)
    pl.semaphore_wait(barrier, heard)

    over, across, cross = range(len(LINE_STEPS), len(LINE_STEPS) + 3)
    other_stage = stage + 1 - 2 * (stage % 2)
    targets = tuple((stage, at(line + step, side, core)) for step in LINE_STEPS) + (
        (stage, at(line, 1 - side, core)),
        (stage, at(line, side, 1 - core)),
        (other_stage, me),
    )

    def copy_of(a, shard, way, receiving=False):
        ref = bufs[a].at[shard]
        if shared(a) and way != across and (way in (over, cross) or shared(a) == 2):
            half = stage % 2
            if receiving and way == cross:
                half = 1 - half
            rows = bufs[a].shape[1] // 2
            ref = bufs[a].at[shard, pl.ds(pl.multiple_of(half * rows, rows), rows)]
        return pltpu.make_async_remote_copy(
            src_ref=ref,
            dst_ref=ref,
            send_sem=send_sem.at[a, way, shard],
            recv_sem=recv_sem.at[a, 1 if way == cross else 0, shard],
            device_id=targets[way],
            device_id_type=MESH,
        )

    def shared(a):
        return SPLIT[a] if stages % 2 == 0 else 0

    def arrived(a, shard, way=across):
        copy_of(a, shard, way, True).wait_recv()

    def along_line(a, source, d, act):
        shard = at(source, side, core)
        for way, step in enumerate(LINE_STEPS):
            here = line + step
            ok = (here >= 0) & (here < line_len)
            if d:
                ok = ok & ((source < line) if step > 0 else (source > line))

            @pl.when(ok)
            def _(way=way):
                act(copy_of(a, shard, way))

    def line_stage(a, d):
        if d == 0:
            loads[a].wait()

        def one(source):
            shard = at(source, side, core)
            if d:
                arrived(a, shard, 0)
            if d % REACH == 0:
                along_line(a, source, d, lambda copy: copy.start())
            copy_of(a, shard, over).start()
            if d and shared(a) == 2:
                copy_of(a, shard, cross).start()
            else:
                copy_of(a, shard, across).start()

        guarded(d, one)

    def sources_of(d):
        if d == 0:
            return [(line, None)]
        return [
            (line + s * d, (line + s * d >= 0) & (line + s * d < line_len)) for s in (-1, 1)
        ]

    def guarded(d, what):
        for source, ok in sources_of(d):
            if ok is None:
                what(source)
            else:
                pl.when(ok)(functools.partial(what, source))

    def side_stage(a, d):
        def one(source):
            shard = at(source, 1 - side, core)
            arrived(a, shard, over)
            copy_of(a, shard, cross if shared(a) else across).start()

        guarded(d, one)

    def cross_stage(a, d):
        def one(source):
            shard = at(source, 1 - side, core)
            if d and shared(a) == 2:
                arrived(a, at(source, side, core), cross)
                copy_of(a, at(source, side, core), across).start()
            arrived(a, shard, cross)
            copy_of(a, shard, across).start()

        if shared(a):
            guarded(d, one)

    def core_stage(a, d):
        def one(source):
            arrived(a, at(source, side, 1 - core))
            arrived(a, at(source, 1 - side, 1 - core))
            base = source * GROUP
            if a == 2:
                rows = valid.shape[1] * GROUP
                part = valid[pl.ds(base, GROUP)].astype(jnp.float32)
                valid_full[pl.ds(pl.multiple_of(source * rows, rows), rows)] = part.reshape(
                    rows, valid.shape[2]
                ).astype(jnp.bfloat16)
                return
            acc, data, buf = (grad_acc, inc, pout) if a == 0 else (act_acc, acts, pin)
            width = buf.shape[2]
            total = acc[...]
            for j in range(GROUP):
                columns = pl.ds(pl.multiple_of((base + j) * width, width), width)
                total += lax.dot_general(
                    buf[base + j], data[:, columns], (((1,), (1,)), ((), ())),
                    preferred_element_type=jnp.float32,
                )
            acc[...] = total

        if d == 0 and a < 2:
            loads[3 + a].wait()
        guarded(d, one)

    def pipe_copy(k):
        return pltpu.make_async_remote_copy(
            src_ref=grad_acc,
            dst_ref=higher.at[k - 1],
            send_sem=pipe_send.at[k - 1],
            recv_sem=pipe_recv.at[k - 1],
            device_id=(stage - k, me),
            device_id_type=MESH,
        )

    steps = [(a, d) for a in range(3) for d in range(line_len)]
    events = sorted(
        (turn(step, shared(step[0]), kind), kind, step) for step in steps for kind in range(4)
    )
    for _, kind, step in events:
        (line_stage, side_stage, cross_stage, core_stage)[kind](*step)
        if kind == 3 and step == (0, line_len - 1):
            for k in range(1, stages):
                @pl.when(stage >= k)
                def _(k=k):
                    pipe_copy(k).start()

    grad = grad_acc[...]
    for k in range(1, stages):
        @pl.when(stage + k < stages)
        def _(k=k):
            pipe_copy(k).wait_recv()

        grad += jnp.where(stage + k < stages, higher[k - 1], 0.0)
    tokens = grad.shape[1]
    size = grad.shape[0]
    live = lengths[0]
    positions = lax.broadcasted_iota(jnp.int32, (1, tokens), 1)
    weights = jnp.where(positions < live, 1.0, 0.0) / jnp.full(
        (1, tokens), live.astype(jnp.float32), jnp.float32
    )
    scaled = grad * weights
    act = act_acc[...]
    row = lax.dot_general(
        scaled, jnp.concatenate([act, act], axis=0), (((1,), (1,)), ((), ())),
        precision=HIGHEST, preferred_element_type=jnp.float32,
    )
    a_index = lax.broadcasted_iota(jnp.int32, (size, 2 * size), 0)
    half = lax.broadcasted_iota(jnp.int32, (size, 2 * size), 1) // size
    for k in range(size // 2):
        wide[:, 2 * size * k : 2 * size * (k + 1)] = jnp.where(
            a_index == 2 * k + half, row, 0.0
        ).astype(jnp.bfloat16)
    terms = lax.dot_general(
        wide[...], valid_full[...], (((1,), (1,)), ((), ())), preferred_element_type=jnp.float32
    )
    scores[me] = jnp.sum(terms, axis=0, keepdims=True)

    def score_copy(k):
        return pltpu.make_async_remote_copy(
            src_ref=scores.at[me],
            dst_ref=scores.at[me],
            send_sem=score_send.at[k],
            recv_sem=score_recv.at[me],
            device_id=(stage, (me + k) % dp),
            device_id_type=MESH,
        )

    for k in range(1, dp):
        score_copy(k).start()
    for k in range(1, dp):
        peer = (me + k) % dp
        pltpu.make_async_remote_copy(
            src_ref=scores.at[peer],
            dst_ref=scores.at[peer],
            send_sem=score_send.at[k],
            recv_sem=score_recv.at[peer],
            device_id=(stage, peer),
            device_id_type=MESH,
        ).wait_recv()
    for e in range(dp):
        line_e = scores[e]
        flat[e : e + 1, :] = line_e
        kept[e : e + 1, :] = line_e * jnp.where(domains[e] == me, 1.0, 0.0)
    gram_ref[0, 0] = lax.dot_general(
        kept[...], flat[...], (((0,), (0,)), ((), ())), precision=HIGHEST,
        preferred_element_type=jnp.float32,
    )

    for k in range(1, dp):
        score_copy(k).wait_send()
    for k in range(1, stages):
        @pl.when(stage >= k)
        def _(k=k):
            pipe_copy(k).wait_send()

    for a, d in steps:
        def sent(source, a=a, d=d):
            mine = at(source, side, core)
            beside = at(source, 1 - side, core)
            if d % REACH == 0:
                along_line(a, source, d, lambda copy: copy.wait_send())
            copy_of(a, mine, over).wait_send()
            copy_of(a, mine, across).wait_send()
            if shared(a):
                copy_of(a, beside, cross).wait_send()
            if d and shared(a) == 2:
                copy_of(a, mine, cross).wait_send()
            copy_of(a, beside, across).wait_send()

        guarded(d, sent)


def solution(mesh):
    stages, dp = mesh.shape["pipe"], mesh.shape["dp"]

    def body(acts, incoming, proj_in, proj_out, valid_rows, lengths, domains):
        tokens, wide = acts.shape[1:]
        size, shard = proj_in.shape
        held, entries = valid_rows.shape[1:]
        queries = held * dp
        any_spec = pl.BlockSpec(memory_space=pl.ANY)
        smem = pl.BlockSpec(memory_space=pltpu.SMEM)
        f32, bf16 = jnp.float32, jnp.bfloat16
        dma = pltpu.SemaphoreType.DMA
        return pl.pallas_call(
            functools.partial(kernel, stages, dp),
            out_shape=jax.ShapeDtypeStruct((1, 1, queries, queries), f32),
            in_specs=[any_spec] * 5 + [smem] * 2,
            out_specs=pl.BlockSpec(memory_space=pltpu.VMEM),
            scratch_shapes=[
                pltpu.VMEM((tokens, wide), bf16),
                pltpu.VMEM((tokens, wide), bf16),
                pltpu.VMEM((dp, size, shard), bf16),
                pltpu.VMEM((dp, size, shard), bf16),
                pltpu.VMEM((dp, held, entries), bf16),
                pltpu.VMEM((queries, entries), bf16),
                pltpu.VMEM((size, tokens), f32),
                pltpu.VMEM((size, tokens), f32),
                pltpu.VMEM((max(stages - 1, 1), size, tokens), f32),
                pltpu.VMEM((size, entries), bf16),
                pltpu.VMEM((dp, 1, queries), f32),
                pltpu.VMEM((dp, queries), f32),
                pltpu.VMEM((dp, queries), f32),
                dma((5,)),
                dma((3, len(LINE_STEPS) + 3, dp)),
                dma((3, 2, dp)),
                dma((max(stages - 1, 1),)),
                dma((max(stages - 1, 1),)),
                dma((dp,)),
                dma((dp,)),
            ],
            compiler_params=pltpu.CompilerParams(collective_id=0, has_side_effects=True),
        )(acts, incoming, proj_in, proj_out, valid_rows, lengths, domains)

    placed = (
        P("pipe", "dp", None),
        P("pipe", "dp", None),
        P(None, "dp"),
        P(None, "dp"),
        P("pipe", "dp", None),
        P("dp"),
        P(),
    )
    return jax.shard_map(
        body, mesh=mesh, in_specs=placed, out_specs=P("pipe", "dp", None, None), check_vma=False
    )
```
